512 devices in a mesh: row: 32 (over z, core), col: 16 (over x, y).
Axes of the slice: x: 4, y: 4, z: 16, core: 2. Of those that a mesh axis runs over, the one named last changes fastest.
Arguments:
- factor_a: bfloat16 [16384, 1024], P(('col', 'row')), may hold values from -0.1875 to 0.1875
- factor_b: bfloat16 [16384, 1024], P(('col', 'row')), may hold values from -0.1875 to 0.1875
- factor_c: bfloat16 [16384, 1024], P(('col', 'row')), may hold values from -0.1875 to 0.1875
Outputs:
- grad_a: float32 [16384, 1024], P(('col', 'row'))
- grad_b: float32 [16384, 1024], P(('col', 'row'))
- grad_c: float32 [16384, 1024], P(('col', 'row'))
The draws below stay inside these ranges and needn't reach their ends.
All inputs are finite; a program needn't handle non-finite values.
Results may differ from the reference program's by a relative error of at most 0.0095.
Values may be sent and summed in bfloat16 or wider, within the bound.
A program may use at most 64 MiB of HBM per device.

```python
import jax
import jax.numpy as jnp
from jax import lax

NMAT = 32
RANK = 16384
FT = 1024
N_COL = 16


def level_of(rng, shape, cuts, low, top_value):
    level = 1.0
    for position, shards_of in cuts:
        steps = jax.random.uniform(jax.random.fold_in(jax.random.fold_in(rng, 6), position), (shards_of,), jnp.float32, low / len(cuts), top_value / len(cuts))
        level = level * jnp.repeat(jnp.exp(steps), shape[position] // shards_of).reshape((-1,) + (1,) * (len(shape) - 1 - position))
    return level


def scatter_about(key, dims, scale, reach, split=(), kind=jnp.bfloat16):
    entries = scale * jax.random.normal(key, dims, jnp.float32)
    if split:
        entries = entries * level_of(key, dims, split, -0.22, 0.18)
    return jnp.clip(entries, -reach, reach).astype(kind)


def setup_inputs(seed: int = 0) -> dict:
    arg_keys = jax.random.split(jax.random.key(seed), 4)
    factor_a = scatter_about(arg_keys[0], (RANK, FT), FT ** -0.5, 0.1875, ((0, 512),))
    factor_b = scatter_about(arg_keys[1], (RANK, FT), FT ** -0.5, 0.1875, ((0, 512),))
    factor_c = scatter_about(arg_keys[2], (RANK, FT), FT ** -0.5, 0.1875, ((0, 512),))
    return dict(factor_a=factor_a, factor_b=factor_b, factor_c=factor_c)


def reference(factor_a, factor_b, factor_c):
    width = RANK // N_COL
    factors = (factor_a, factor_b, factor_c)

    def one_block(carry, index):
        start = (index * width).astype(jnp.int32)
        pieces = [lax.dynamic_slice_in_dim(f, start, width, 0) for f in factors]
        grams = [lax.dot_general(p, f, (((1,), (1,)), ((), ())), preferred_element_type=jnp.float32) for p, f in zip(pieces, factors)]
        hadam_a = (grams[1] * grams[2]).astype(jnp.bfloat16)
        hadam_b = (grams[2] * grams[0]).astype(jnp.bfloat16)
        hadam_c = (grams[0] * grams[1]).astype(jnp.bfloat16)
        hadams = (hadam_a, hadam_b, hadam_c)
        parts = [lax.dot_general(h, p, (((0,), (0,)), ((), ())), preferred_element_type=jnp.float32).astype(jnp.bfloat16) for p, h in zip(pieces, hadams)]
        new_carry = tuple(c + q.astype(jnp.float32) for c, q in zip(carry, parts))
        return new_carry, None

    zeros = jnp.zeros((RANK, FT), jnp.float32)
    summed, _ = lax.scan(one_block, (zeros, zeros, zeros), jnp.arange(N_COL, dtype=jnp.int32))
    cube_a = factor_a.astype(jnp.float32).reshape(RANK, NMAT, NMAT)
    cube_b = factor_b.astype(jnp.float32).reshape(RANK, NMAT, NMAT)
    cube_c = factor_c.astype(jnp.float32).reshape(RANK, NMAT, NMAT)
    data_a = jnp.einsum('rjk,rki->rij', cube_b, cube_c).reshape(RANK, FT)
    data_b = jnp.einsum('rki,rij->rjk', cube_c, cube_a).reshape(RANK, FT)
    data_c = jnp.einsum('rij,rjk->rki', cube_a, cube_b).reshape(RANK, FT)
    grad_a = NMAT * (summed[0] - data_a)
    grad_b = NMAT * (summed[1] - data_b)
    grad_c = NMAT * (summed[2] - data_c)
    return (grad_a, grad_b, grad_c)
```

```python
import jax
import jax.numpy as jnp
from jax import lax
from jax.experimental import pallas as pl
from jax.experimental.pallas import tpu as pltpu
from jax.sharding import PartitionSpec as P

NMAT = 32
MESH = pl.DeviceIdType.MESH
SUB = 16
STEPS = 15


def gram(left, right):
    return lax.dot_general(left, right, (((1,), (1,)), ((), ())), preferred_element_type=jnp.float32)


def pair_kernel(
    a_hbm, b_hbm, c_hbm, out_ref,
    jbuf, ibuf, acc, stage_b, recv_b, stage_a, recv_a,
    load_sem, z_send, z_recv, s_send, s_recv, ga_send, ga_recv, gb_send, gb_recv, rb_send, rb_recv, ra_send, ra_recv,
):
    row, col = lax.axis_index("row"), lax.axis_index("col")
    z, core = row // 2, lax.rem(row, 2)
    x, y = col // 4, lax.rem(col, 4)
    sign = 1 - 2 * core
    z_next = (lax.rem(z + 1, 16) * 2 + core, col)
    z_prev = (lax.rem(z + 15, 16) * 2 + core, col)
    sibling = (z * 2 + 1 - core, col)
    x_fwd = (row, lax.rem(x + 4 + sign, 4) * 4 + y)
    x_back = (row, lax.rem(x + 4 - sign, 4) * 4 + y)
    y_fwd = (row, x * 4 + lax.rem(y + 4 + sign, 4))
    y_back = (row, x * 4 + lax.rem(y + 4 - sign, 4))
    first = ((x_fwd, x_back), (y_fwd, y_back))
    second = ((y_fwd, y_back), (x_fwd, x_back))

    loads = [pltpu.make_async_copy(f, jbuf.at[i, pl.ds(0, 32)], load_sem.at[i]) for i, f in enumerate((a_hbm, b_hbm, c_hbm))]
    for load in loads:
        load.start()
    barrier = pltpu.get_barrier_semaphore()
    partners = (z_next, z_prev, sibling, x_fwd, x_back, y_fwd, y_back)
    for p in partners:
        pl.semaphore_signal(barrier, inc=1, device_id=p, device_id_type=MESH)
    for load in loads:
        load.wait()
    pl.semaphore_wait(barrier, len(partners))

    started = []

    def copy(src, dst, send, recv, device):
        return pltpu.make_async_remote_copy(src, dst, send, recv, device_id=device, device_id_type=MESH)

    def go(c):
        c.start()
        started.append(c)

    def jrows(slot, n=SUB):
        return jbuf.at[:, pl.ds(slot * SUB, n)]

    def z_copy(k, d):
        if k <= 2:
            src = k - 1 if d == 0 else 2 - k
        else:
            src = 4 * (k - 2) + d
        return copy(jrows(src), jrows(4 * k + d), z_send.at[d, k], z_recv.at[d, k], (z_next, z_prev)[d])

    def s_copy(k, d):
        return copy(jrows(4 * k + d), jrows(4 * k + 2 + d), s_send.at[d, k], s_recv.at[d, k], sibling)

    own_copy = copy(jrows(0, 32), jrows(2, 32), s_send.at[0, 0], s_recv.at[0, 0], sibling)

    def irows(t, slot):
        return ibuf.at[t, :, pl.ds(slot * SUB, SUB)]

    def ga_copy(t, kind):
        fwd, back = first[t]
        own = jrows(t)
        src, slot, device = ((own, 3, fwd), (own, 1, back), (irows(t, 3), 2, fwd))[kind]
        return copy(src, irows(t, slot), ga_send.at[t, kind], ga_recv.at[t, kind], device)

    def gb_copy(t, kind, a):
        fwd, back = second[t]
        own = jrows(t) if a == 0 else irows(t, a)
        src, b, device = ((own, 3, fwd), (own, 1, back), (irows(t, 12 + a), 2, fwd))[kind]
        return copy(src, irows(t, 4 * b + a), gb_send.at[t, kind, a], gb_recv.at[t, kind, a], device)

    def rb_copy(t, f, kind):
        fwd, back = second[t]
        return copy(stage_b.at[t, f, kind], recv_b.at[t, f, kind], rb_send.at[t, f, kind], rb_recv.at[t, f, kind], (fwd, back, fwd)[kind])

    def ra_copy(t, f, kind):
        fwd, back = first[t]
        return copy(stage_a.at[t, f, kind], recv_a.at[t, f, kind], ra_send.at[t, f, kind], ra_recv.at[t, f, kind], (fwd, back, fwd)[kind])

    def unit(t, group, last=False):
        rights = [jbuf[f, pl.ds(group * 256, 256)] for f in range(3)]
        grams = [gram(ibuf[t, f], rights[f]) for f in range(3)]
        hadams = [(grams[(f + 1) % 3] * grams[(f + 2) % 3]).astype(jnp.bfloat16) for f in range(3)]
        for f in range(3):
            term = jnp.dot(hadams[f], rights[f], preferred_element_type=jnp.float32)
            if group > 0:
                term = acc[t, f] + term
            if last:
                stage_b[t, f, 0] = term[128:192].astype(jnp.bfloat16)
                stage_b[t, f, 1] = term[192:256].astype(jnp.bfloat16)
                go(rb_copy(t, f, 0))
                go(rb_copy(t, f, 1))
                acc[t, f, pl.ds(0, 128)] = term[0:128]
            else:
                acc[t, f] = term

    def wait_group(group):
        for k in range(4 * group, 4 * group + 4):
            if k == 0:
                own_copy.wait_recv()
            else:
                s_copy(k, 0).wait_recv()
                s_copy(k, 1).wait_recv()

    for k in (1, 2):
        for d in range(2):
            go(z_copy(k, d))
    for t in range(2):
        go(ga_copy(t, 0))
        go(ga_copy(t, 1))
        go(gb_copy(t, 0, 0))
        go(gb_copy(t, 1, 0))
    go(own_copy)
    for t in range(2):
        ibuf[t, :, pl.ds(0, SUB)] = jbuf[:, pl.ds(t * SUB, SUB)]

    work = {9: [(0, 0)], 10: [(1, 0)], 11: [(0, 1)], 12: [(1, 1)], 13: [(0, 2)], 14: [(1, 2)]}
    for k in range(1, STEPS + 1):
        for d in range(2):
            z_copy(k, d).wait_recv()
            if k + 2 <= STEPS:
                go(z_copy(k + 2, d))
            go(s_copy(k, d))
        if k == 1:
            for t in range(2):
                ga_copy(t, 0).wait_recv()
                go(ga_copy(t, 2))
                go(gb_copy(t, 0, 3))
                go(gb_copy(t, 1, 3))
                ga_copy(t, 1).wait_recv()
                go(gb_copy(t, 0, 1))
                go(gb_copy(t, 1, 1))
        if k == 2:
            for t in range(2):
                ga_copy(t, 2).wait_recv()
                go(gb_copy(t, 0, 2))
                go(gb_copy(t, 1, 2))
                gb_copy(t, 0, 0).wait_recv()
                go(gb_copy(t, 2, 0))
        for a, when in ((3, 4), (1, 5), (2, 7)):
            if k == when:
                for t in range(2):
                    gb_copy(t, 0, a).wait_recv()
                    go(gb_copy(t, 2, a))
        if k == 9:
            for t in range(2):
                for a in range(4):
                    gb_copy(t, 1, a).wait_recv()
                    gb_copy(t, 2, a).wait_recv()
        for t, group in work.get(k, ()):
            if t == 0:
                wait_group(group)
            unit(t, group)
    wait_group(3)
    for t in range(2):
        unit(t, 3, last=True)

    for t in range(2):
        for f in range(3):
            rb_copy(t, f, 0).wait_recv()
            stage_b[t, f, 2] = (acc[t, f, pl.ds(64, 64)] + recv_b[t, f, 0].astype(jnp.float32)).astype(jnp.bfloat16)
            go(rb_copy(t, f, 2))
    for t in range(2):
        for f in range(3):
            rb_copy(t, f, 1).wait_recv()
            rb_copy(t, f, 2).wait_recv()
            total = acc[t, f, pl.ds(0, 64)] + recv_b[t, f, 1].astype(jnp.float32) + recv_b[t, f, 2].astype(jnp.float32)
            stage_a[t, f, 0] = total[32:48].astype(jnp.bfloat16)
            stage_a[t, f, 1] = total[48:64].astype(jnp.bfloat16)
            go(ra_copy(t, f, 0))
            go(ra_copy(t, f, 1))
            acc[t, f, pl.ds(0, 32)] = total[0:32]
    for t in range(2):
        for f in range(3):
            ra_copy(t, f, 0).wait_recv()
            stage_a[t, f, 2] = (acc[t, f, pl.ds(16, 16)] + recv_a[t, f, 0].astype(jnp.float32)).astype(jnp.bfloat16)
            go(ra_copy(t, f, 2))
    for t in range(2):
        for f in range(3):
            ra_copy(t, f, 1).wait_recv()
            ra_copy(t, f, 2).wait_recv()
            out_ref[f, pl.ds(t * SUB, SUB)] = (
                acc[t, f, pl.ds(0, 16)] + recv_a[t, f, 1].astype(jnp.float32) + recv_a[t, f, 2].astype(jnp.float32)
            )
    for c in started:
        c.wait_send()


def pair_sums(factor_a, factor_b, factor_c):
    dma = pltpu.SemaphoreType.DMA
    return pl.pallas_call(
        pair_kernel,
        out_shape=jax.ShapeDtypeStruct((3, 32, 1024), jnp.float32),
        in_specs=[pl.BlockSpec(memory_space=pl.ANY)] * 3,
        out_specs=pl.BlockSpec(memory_space=pltpu.VMEM),
        scratch_shapes=[
            pltpu.VMEM((3, 1024, 1024), jnp.bfloat16),
            pltpu.VMEM((2, 3, 256, 1024), jnp.bfloat16),
            pltpu.VMEM((2, 3, 256, 1024), jnp.float32),
            pltpu.VMEM((2, 3, 3, 64, 1024), jnp.bfloat16),
            pltpu.VMEM((2, 3, 3, 64, 1024), jnp.bfloat16),
            pltpu.VMEM((2, 3, 3, 16, 1024), jnp.bfloat16),
            pltpu.VMEM((2, 3, 3, 16, 1024), jnp.bfloat16),
            dma((3,)), dma((2, 16)), dma((2, 16)), dma((2, 16)), dma((2, 16)),
            dma((2, 3)), dma((2, 3)), dma((2, 3, 4)), dma((2, 3, 4)),
            dma((2, 3, 3)), dma((2, 3, 3)), dma((2, 3, 3)), dma((2, 3, 3)),
        ],
        compiler_params=pltpu.CompilerParams(collective_id=0, has_side_effects=True, vmem_limit_bytes=56 * 1024 * 1024),
        cost_estimate=pl.CostEstimate(flops=6 * 2 * 512 * 1024 * 1024, bytes_accessed=1 << 20, transcendentals=0),
        name="pair_sums",
    )(factor_a, factor_b, factor_c)


def shards(factor_a, factor_b, factor_c):
    own_rows, length = factor_a.shape
    summed = pair_sums(factor_a, factor_b, factor_c)
    cube_a = factor_a.astype(jnp.float32).reshape(own_rows, NMAT, NMAT)
    cube_b = factor_b.astype(jnp.float32).reshape(own_rows, NMAT, NMAT)
    cube_c = factor_c.astype(jnp.float32).reshape(own_rows, NMAT, NMAT)
    data_a = jnp.einsum("rjk,rki->rij", cube_b, cube_c).reshape(own_rows, length)
    data_b = jnp.einsum("rki,rij->rjk", cube_c, cube_a).reshape(own_rows, length)
    data_c = jnp.einsum("rij,rjk->rki", cube_a, cube_b).reshape(own_rows, length)
    return (NMAT * (summed[0] - data_a), NMAT * (summed[1] - data_b), NMAT * (summed[2] - data_c))


def solution(mesh):
    specs = (P(("col", "row"), None),) * 3
    return jax.shard_map(shards, mesh=mesh, in_specs=specs, out_specs=specs, check_vma=False)
```

```python
import jax
import jax.numpy as jnp
from jax import lax
from jax.experimental import pallas as pl
from jax.experimental.pallas import tpu as pltpu
from jax.sharding import PartitionSpec as P

NMAT = 32
MESH = pl.DeviceIdType.MESH
SUB = 16
STEPS = 15


def gram(left, right):
    return lax.dot_general(left, right, (((1,), (1,)), ((), ())), preferred_element_type=jnp.float32)


def pair_kernel(
    a_hbm, b_hbm, c_hbm, *rest,
):
    outs = rest[:3]
    (jbuf, ibuf, acc, grams, trace, stage_b, recv_b, stage_a, recv_a,
    load_sem, z_send, z_recv, s_send, s_recv, ga_send, ga_recv, gb_send, gb_recv, rb_send, rb_recv, ra_send, ra_recv) = rest[3:]
    row, col = lax.axis_index("row"), lax.axis_index("col")
    z, core = row // 2, lax.rem(row, 2)
    x, y = col // 4, lax.rem(col, 4)
    sign = 1 - 2 * core
    z_next = (lax.rem(z + 1, 16) * 2 + core, col)
    z_prev = (lax.rem(z + 15, 16) * 2 + core, col)
    sibling = (z * 2 + 1 - core, col)
    x_fwd = (row, lax.rem(x + 4 + sign, 4) * 4 + y)
    x_back = (row, lax.rem(x + 4 - sign, 4) * 4 + y)
    y_fwd = (row, x * 4 + lax.rem(y + 4 + sign, 4))
    y_back = (row, x * 4 + lax.rem(y + 4 - sign, 4))
    x_far = (row, lax.rem(x + 2, 4) * 4 + y)
    y_far = (row, x * 4 + lax.rem(y + 2, 4))
    far = (x_far, y_far)
    first = ((x_fwd, x_back), (y_fwd, y_back))
    second = ((y_fwd, y_back), (x_fwd, x_back))

    loads = [pltpu.make_async_copy(f, jbuf.at[i, pl.ds(0, 32)], load_sem.at[i]) for i, f in enumerate((a_hbm, b_hbm, c_hbm))]
    for load in loads:
        load.start()
    barrier = pltpu.get_barrier_semaphore()
    partners = (z_next, z_prev, sibling, x_fwd, x_back, y_fwd, y_back, x_far, y_far)
    for p in partners:
        pl.semaphore_signal(barrier, inc=1, device_id=p, device_id_type=MESH)
    for load in loads:
        load.wait()
    pl.semaphore_wait(barrier, len(partners))

    sent = []

    def copy(src, dst, send, recv, device):
        return pltpu.make_async_remote_copy(src, dst, send, recv, device_id=device, device_id_type=MESH)

    def go(c):
        c.start()
        sent.append(c)

    def jrows(slot, n=SUB):
        return jbuf.at[:, pl.ds(slot * SUB, n)]

    def z_copy(k, f, d):
        if k <= 2:
            src = k - 1 if d == 0 else 2 - k
        else:
            src = 4 * (k - 2) + d
        return copy(
            jbuf.at[f, pl.ds(src * SUB, SUB)], jbuf.at[f, pl.ds((4 * k + d) * SUB, SUB)],
            z_send.at[d, k, f], z_recv.at[d, k, f], (z_next, z_prev)[d],
        )

    def s_copy(k, d):
        return copy(jrows(4 * k + d), jrows(4 * k + 2 + d), s_send.at[d, k], s_recv.at[d, k], sibling)

    own_copy = copy(jrows(0, 2 * SUB), jrows(2, 2 * SUB), s_send.at[0, 0], s_recv.at[0, 0], sibling)

    def irows(t, slot):
        return ibuf.at[t, :, pl.ds(slot * SUB, SUB)]

    def ga_copy(t, kind):
        fwd, back = first[t]
        own = jrows(t)
        src, slot, device = ((own, 3, fwd), (own, 1, back), (irows(t, 3), 2, fwd))[kind]
        return copy(src, irows(t, slot), ga_send.at[t, kind], ga_recv.at[t, kind], device)

    def gb_copy(t, kind, a):
        fwd, back = second[t]
        own = jrows(t) if a == 0 else irows(t, a)
        src, b, device = ((own, 3, fwd), (own, 1, back), (irows(t, 12 + a), 2, fwd))[kind]
        return copy(src, irows(t, 4 * b + a), gb_send.at[t, kind, a], gb_recv.at[t, kind, a], device)

    def rb_copy(t, f, kind):
        fwd, back = second[t]
        return copy(stage_b.at[t, f, kind], recv_b.at[t, f, kind], rb_send.at[t, f, kind], rb_recv.at[t, f, kind], (fwd, back, fwd)[kind])

    def ra_copy(t, f, kind):
        fwd, back = first[t]
        device = (fwd, far[t], back)[kind]
        return copy(stage_a.at[t, f, kind], recv_a.at[t, f, kind], ra_send.at[t, f, kind], ra_recv.at[t, f, kind], device)

    def gram_item(t, group, f):
        def run():
            grams[t, f] = gram(ibuf[t, f], jbuf[f, pl.ds(group * 256, 256)])
        return run

    def apply_item(t, group, f):
        def run():
            hadam = (grams[t, (f + 1) % 3] * grams[t, (f + 2) % 3]).astype(jnp.bfloat16)
            term = jnp.dot(hadam, jbuf[f, pl.ds(group * 256, 256)], preferred_element_type=jnp.float32)
            if group > 0:
                term = acc[t, f] + term
            if group == 3:
                stage_b[t, f, 0] = term[128:192].astype(jnp.bfloat16)
                stage_b[t, f, 1] = term[192:256].astype(jnp.bfloat16)
                go(rb_copy(t, f, 0))
                go(rb_copy(t, f, 1))
                acc[t, f, pl.ds(0, 128)] = term[0:128]
            else:
                acc[t, f] = term
        return run

    def wait_group(group):
        for k in range(4 * group, 4 * group + 4):
            if k == 0:
                own_copy.wait_recv()
            else:
                s_copy(k, 0).wait_recv()
                s_copy(k, 1).wait_recv()

    def unit_items(t, group):
        items = [gram_item(t, group, f) for f in range(3)] + [apply_item(t, group, f) for f in range(3)]
        return items

    for f in range(3):
        for d in range(2):
            go(z_copy(1, f, d))
    for t in range(2):
        go(ga_copy(t, 0))
        go(ga_copy(t, 1))
    for f in range(3):
        for d in range(2):
            go(z_copy(2, f, d))
    for t in range(2):
        go(gb_copy(t, 0, 0))
        go(gb_copy(t, 1, 0))
    go(own_copy)
    for t in range(2):
        ibuf[t, :, pl.ds(0, SUB)] = jbuf[:, pl.ds(t * SUB, SUB)]

    def trace_terms():
        cubes = [jbuf[f, pl.ds(0, 32)].reshape(32, NMAT, NMAT) for f in range(3)]
        for f, spec in enumerate(("rjk,rki->rij", "rki,rij->rjk", "rij,rjk->rki")):
            data = jnp.einsum(spec, cubes[(f + 1) % 3], cubes[(f + 2) % 3] , preferred_element_type=jnp.float32)
            trace[f] = data.reshape(32, NMAT * NMAT)

    ready = {9: 0, 10: 1, 12: 2}
    queue = []

    def xy_events(k):
        if k == ga_at[0]:
            for t in range(2):
                ga_copy(t, 0).wait_recv()
                go(ga_copy(t, 2))
                go(gb_copy(t, 0, 3))
                go(gb_copy(t, 1, 3))
            for t in range(2):
                ga_copy(t, 1).wait_recv()
                go(gb_copy(t, 0, 1))
                go(gb_copy(t, 1, 1))
        if k == ga_at[1]:
            for t in range(2):
                ga_copy(t, 2).wait_recv()
                go(gb_copy(t, 0, 2))
                go(gb_copy(t, 1, 2))
        for a, when in gb_at:
            if k == when:
                for t in range(2):
                    gb_copy(t, 0, a).wait_recv()
                    go(gb_copy(t, 2, a))
        if k == i_at:
            for t in range(2):
                for a in range(4):
                    gb_copy(t, 1, a).wait_recv()
                    gb_copy(t, 2, a).wait_recv()

    ga_at, gb_at, i_at = (2, 4), ((0, 3), (3, 5), (1, 6), (2, 7)), 9
    for k in range(1, STEPS + 1):
        for f in range(3):
            for d in range(2):
                z_copy(k, f, d).wait_recv()
                if k + 2 <= STEPS:
                    go(z_copy(k + 2, f, d))
                if f == 2:
                    go(s_copy(k, d))
            if f == 0:
                xy_events(k)
                if k == 1:
                    trace_terms()
                if k in ready:
                    wait_group(ready[k])
                    queue.extend(unit_items(0, ready[k]) + unit_items(1, ready[k]))
            for _ in range(2):
                if queue:
                    queue.pop(0)()
    while queue:
        queue.pop(0)()
    wait_group(3)
    for item in unit_items(0, 3) + unit_items(1, 3):
        item()

    gathers = sent[:-12]
    reduces = sent[-12:]
    del sent[:]
    for c in gathers:
        c.wait_send()
    for t in range(2):
        for f in range(3):
            rb_copy(t, f, 0).wait_recv()
            stage_b[t, f, 2] = (acc[t, f, pl.ds(64, 64)] + recv_b[t, f, 0].astype(jnp.float32)).astype(jnp.bfloat16)
            go(rb_copy(t, f, 2))
    for t in range(2):
        for f in range(3):
            rb_copy(t, f, 1).wait_recv()
            rb_copy(t, f, 2).wait_recv()
            total = acc[t, f, pl.ds(0, 64)] + recv_b[t, f, 1].astype(jnp.float32) + recv_b[t, f, 2].astype(jnp.float32)
            for kind, a in ((1, 2), (0, 1), (2, 3)):
                stage_a[t, f, kind] = total[SUB * a : SUB * a + SUB].astype(jnp.bfloat16)
                go(ra_copy(t, f, kind))
            acc[t, f, pl.ds(0, SUB)] = total[0:SUB]
    for c in reduces:
        c.wait_send()
    for t in range(2):
        for f, out_ref in enumerate(outs):
            for kind in range(3):
                ra_copy(t, f, kind).wait_recv()
            received = [recv_a[t, f, kind].astype(jnp.float32) for kind in range(3)]
            summed = acc[t, f, pl.ds(0, SUB)] + received[0] + received[1] + received[2]
            out_ref[pl.ds(t * SUB, SUB)] = NMAT * (summed - trace[f, pl.ds(t * SUB, SUB)])
    for c in sent:
        c.wait_send()


def pair_sums(factor_a, factor_b, factor_c):
    dma = pltpu.SemaphoreType.DMA
    return pl.pallas_call(
        pair_kernel,
        out_shape=[jax.ShapeDtypeStruct((32, 1024), jnp.float32)] * 3,
        in_specs=[pl.BlockSpec(memory_space=pl.ANY)] * 3,
        out_specs=[pl.BlockSpec(memory_space=pltpu.VMEM)] * 3,
        scratch_shapes=[
            pltpu.VMEM((3, 1024, 1024), jnp.bfloat16),
            pltpu.VMEM((2, 3, 256, 1024), jnp.bfloat16),
            pltpu.VMEM((2, 3, 256, 1024), jnp.float32),
            pltpu.VMEM((2, 3, 256, 256), jnp.float32),
            pltpu.VMEM((3, 32, 1024), jnp.float32),
            pltpu.VMEM((2, 3, 3, 64, 1024), jnp.bfloat16),
            pltpu.VMEM((2, 3, 3, 64, 1024), jnp.bfloat16),
            pltpu.VMEM((2, 3, 3, 16, 1024), jnp.bfloat16),
            pltpu.VMEM((2, 3, 3, 16, 1024), jnp.bfloat16),
            dma((3,)), dma((2, 16, 3)), dma((2, 16, 3)), dma((2, 16)), dma((2, 16)),
            dma((2, 3)), dma((2, 3)), dma((2, 3, 4)), dma((2, 3, 4)),
            dma((2, 3, 3)), dma((2, 3, 3)), dma((2, 3, 3)), dma((2, 3, 3)),
        ],
        compiler_params=pltpu.CompilerParams(collective_id=0, has_side_effects=True, vmem_limit_bytes=56 * 1024 * 1024),
        cost_estimate=pl.CostEstimate(flops=6 * 2 * 512 * 1024 * 1024, bytes_accessed=1 << 20, transcendentals=0),
        name="pair_sums",
    )(factor_a, factor_b, factor_c)


def shards(factor_a, factor_b, factor_c):
    return tuple(pair_sums(factor_a, factor_b, factor_c))


def solution(mesh):
    specs = (P(("col", "row"), None),) * 3
    return jax.shard_map(shards, mesh=mesh, in_specs=specs, out_specs=specs, check_vma=False)
```

```python
import jax
import jax.numpy as jnp
from jax import lax
from jax.experimental import pallas as pl
from jax.experimental.pallas import tpu as pltpu
from jax.sharding import PartitionSpec as P

NMAT = 32
MESH = pl.DeviceIdType.MESH
SUB = 16
STEPS = 15


def gram(left, right):
    return lax.dot_general(left, right, (((1,), (1,)), ((), ())), preferred_element_type=jnp.float32)


def pair_kernel(
    a_hbm, b_hbm, c_hbm, *rest,
):
    outs = [rest[0].at[f] for f in range(3)]
    (jbuf, ibuf, acc, grams, trace, stage_b, recv_b, stage_a, recv_a,
    load_sem, z_send, z_recv, s_send, s_recv, ga_send, ga_recv, gb_send, gb_recv, rb_send, rb_recv, ra_send, ra_recv) = rest[1:]
    row, col = lax.axis_index("row"), lax.axis_index("col")
    z, core = row // 2, lax.rem(row, 2)
    x, y = col // 4, lax.rem(col, 4)
    sign = 1 - 2 * core
    z_next = (lax.rem(z + 1, 16) * 2 + core, col)
    z_prev = (lax.rem(z + 15, 16) * 2 + core, col)
    sibling = (z * 2 + 1 - core, col)
    x_fwd = (row, lax.rem(x + 4 + sign, 4) * 4 + y)
    x_back = (row, lax.rem(x + 4 - sign, 4) * 4 + y)
    y_fwd = (row, x * 4 + lax.rem(y + 4 + sign, 4))
    y_back = (row, x * 4 + lax.rem(y + 4 - sign, 4))
    x_far = (row, lax.rem(x + 2, 4) * 4 + y)
    y_far = (row, x * 4 + lax.rem(y + 2, 4))
    far = (x_far, y_far)
    first = ((x_fwd, x_back), (y_fwd, y_back))
    second = ((y_fwd, y_back), (x_fwd, x_back))

    factors = (a_hbm, b_hbm, c_hbm)
    barrier = pltpu.get_barrier_semaphore()
    partners = (z_next, z_prev, sibling, x_fwd, x_back, y_fwd, y_back, x_far, y_far)
    for p in partners:
        pl.semaphore_signal(barrier, inc=1, device_id=p, device_id_type=MESH)
    loads = [pltpu.make_async_copy(factors[f], jbuf.at[f, pl.ds(0, 2 * SUB)], load_sem.at[f]) for f in range(3)]
    for load in loads:
        load.start()
    pl.semaphore_wait(barrier, len(partners))

    sent = []

    def copy(src, dst, send, recv, device):
        return pltpu.make_async_remote_copy(src, dst, send, recv, device_id=device, device_id_type=MESH)

    def go(c):
        c.start()
        sent.append(c)

    def jrows(slot, n=SUB):
        return jbuf.at[:, pl.ds(slot * SUB, n)]

    def z_copy(k, f, d):
        if k <= 2:
            src = factors[f].at[pl.ds((k - 1 if d == 0 else 2 - k) * SUB, SUB)]
        else:
            src = jbuf.at[f, pl.ds((4 * (k - 2) + d) * SUB, SUB)]
        return copy(
            src, jbuf.at[f, pl.ds((4 * k + d) * SUB, SUB)],
            z_send.at[d, k, f], z_recv.at[d, k, f], (z_next, z_prev)[d],
        )

    def s_copy(k, d):
        return copy(jrows(4 * k + d), jrows(4 * k + 2 + d), s_send.at[d, k], s_recv.at[d, k], sibling)

    own_copy = copy(jrows(0, 2 * SUB), jrows(2, 2 * SUB), s_send.at[0, 0], s_recv.at[0, 0], sibling)

    def irows(t, slot):
        return ibuf.at[t, :, pl.ds(slot * SUB, SUB)]

    def ga_copy(t, kind):
        fwd, back = first[t]
        own = jrows(t)
        src, slot, device = ((own, 3, fwd), (own, 1, back), (irows(t, 3), 2, fwd))[kind]
        return copy(src, irows(t, slot), ga_send.at[t, kind], ga_recv.at[t, kind], device)

    def gb_copy(t, kind, a):
        fwd, back = second[t]
        own = jrows(t) if a == 0 else irows(t, a)
        src, b, device = ((own, 3, fwd), (own, 1, back), (irows(t, 12 + a), 2, fwd))[kind]
        return copy(src, irows(t, 4 * b + a), gb_send.at[t, kind, a], gb_recv.at[t, kind, a], device)

    def rb_copy(t, f, kind):
        fwd, back = second[t]
        return copy(stage_b.at[t, f, kind], recv_b.at[t, f, kind], rb_send.at[t, f, kind], rb_recv.at[t, f, kind], (fwd, back, fwd)[kind])

    def ra_copy(t, f, kind):
        fwd, back = first[t]
        device = (fwd, far[t], back)[kind]
        return copy(stage_a.at[t, f, kind], recv_a.at[t, f, kind], ra_send.at[t, f, kind], ra_recv.at[t, f, kind], device)

    def gram_item(t, group, f):
        def run():
            grams[t, f] = gram(ibuf[t, f], jbuf[f, pl.ds(group * 256, 256)])
        return run

    def apply_item(t, group, f):
        def run():
            hadam = (grams[t, (f + 1) % 3] * grams[t, (f + 2) % 3]).astype(jnp.bfloat16)
            term = jnp.dot(hadam, jbuf[f, pl.ds(group * 256, 256)], preferred_element_type=jnp.float32)
            if group > 0:
                term = acc[t, f] + term
            if group == 3:
                stage_b[t, f, 0] = term[128:192].astype(jnp.bfloat16)
                stage_b[t, f, 1] = term[192:256].astype(jnp.bfloat16)
                go(rb_copy(t, f, 0))
                acc[t, f, pl.ds(0, 128)] = term[0:128]
            else:
                acc[t, f] = term
        return run

    def wait_group(group):
        for k in range(4 * group, 4 * group + 4):
            if k == 0:
                own_copy.wait_recv()
            else:
                s_copy(k, 0).wait_recv()
                s_copy(k, 1).wait_recv()

    def unit_items(t, group):
        items = [gram_item(t, group, f) for f in range(3)] + [apply_item(t, group, f) for f in range(3)]
        return items

    for f in range(3):
        for d in range(2):
            go(z_copy(1, f, d))
    for load in loads:
        load.wait()
    for t in range(2):
        go(ga_copy(t, 0))
        go(ga_copy(t, 1))
    for f in range(3):
        for d in range(2):
            go(z_copy(2, f, d))
    for t in range(2):
        go(gb_copy(t, 0, 0))
        go(gb_copy(t, 1, 0))
    go(own_copy)
    for t in range(2):
        ibuf[t, :, pl.ds(0, SUB)] = jbuf[:, pl.ds(t * SUB, SUB)]

    def trace_terms():
        cubes = [jbuf[f, pl.ds(0, 32)].reshape(32, NMAT, NMAT) for f in range(3)]
        for f, spec in enumerate(("rjk,rki->rij", "rki,rij->rjk", "rij,rjk->rki")):
            data = jnp.einsum(spec, cubes[(f + 1) % 3], cubes[(f + 2) % 3] , preferred_element_type=jnp.float32)
            trace[f] = data.reshape(32, NMAT * NMAT)

    ready = {9: 0, 10: 1, 12: 2}
    queue = []

    def xy_events(k):
        if k == ga_at[0]:
            for t in range(2):
                ga_copy(t, 0).wait_recv()
                go(ga_copy(t, 2))
                go(gb_copy(t, 0, 3))
                go(gb_copy(t, 1, 3))
            for t in range(2):
                ga_copy(t, 1).wait_recv()
                go(gb_copy(t, 0, 1))
                go(gb_copy(t, 1, 1))
        if k == ga_at[1]:
            for t in range(2):
                ga_copy(t, 2).wait_recv()
                go(gb_copy(t, 0, 2))
                go(gb_copy(t, 1, 2))
        for a, when in gb_at:
            if k == when:
                for t in range(2):
                    gb_copy(t, 0, a).wait_recv()
                    go(gb_copy(t, 2, a))
        if k == i_at:
            for t in range(2):
                for a in range(4):
                    gb_copy(t, 1, a).wait_recv()
                    gb_copy(t, 2, a).wait_recv()

    ga_at, gb_at, i_at = (2, 4), ((0, 3), (3, 5), (1, 6), (2, 7)), 9
    for k in range(1, STEPS + 1):
        for f in range(3):
            for d in range(2):
                z_copy(k, f, d).wait_recv()
                if k + 2 <= STEPS:
                    go(z_copy(k + 2, f, d))
                if f == 2:
                    go(s_copy(k, d))
            if f == 0:
                xy_events(k)
                if k == 1:
                    trace_terms()
                if k in ready:
                    wait_group(ready[k])
                    queue.extend(unit_items(0, ready[k]) + unit_items(1, ready[k]))
            for _ in range(2):
                if queue:
                    queue.pop(0)()
    while queue:
        queue.pop(0)()
    wait_group(3)
    gathers = list(sent)
    del sent[:]
    for f in (1, 2):
        gram_item(0, 3, f)()
    apply_item(0, 3, 0)()
    for f in (1, 2):
        gram_item(1, 3, f)()
    apply_item(1, 3, 0)()
    for t in range(2):
        gram_item(t, 3, 0)()
        apply_item(t, 3, 1)()
    for t in range(2):
        apply_item(t, 3, 2)()
    for c in gathers:
        c.wait_send()
    for f in range(3):
        for t in range(2):
            rb_copy(t, f, 0).wait_recv()
            stage_b[t, f, 2] = (acc[t, f, pl.ds(64, 64)] + recv_b[t, f, 0].astype(jnp.float32)).astype(jnp.bfloat16)
            go(rb_copy(t, f, 2))
            go(rb_copy(t, f, 1))
    for f in range(3):
        for t in range(2):
            rb_copy(t, f, 1).wait_recv()
            rb_copy(t, f, 2).wait_recv()
            total = acc[t, f, pl.ds(0, 64)] + recv_b[t, f, 1].astype(jnp.float32) + recv_b[t, f, 2].astype(jnp.float32)
            for kind, a in ((1, 2), (0, 1), (2, 3)):
                stage_a[t, f, kind] = total[SUB * a : SUB * a + SUB].astype(jnp.bfloat16)
                go(ra_copy(t, f, kind))
            acc[t, f, pl.ds(0, SUB)] = total[0:SUB]
    for c in sent[:18]:
        c.wait_send()
    del sent[:18]
    for f, out_ref in enumerate(outs):
        for t in range(2):
            for kind in range(3):
                ra_copy(t, f, kind).wait_recv()
            received = [recv_a[t, f, kind].astype(jnp.float32) for kind in range(3)]
            summed = acc[t, f, pl.ds(0, SUB)] + received[0] + received[1] + received[2]
            out_ref[pl.ds(t * SUB, SUB)] = summed - trace[f, pl.ds(t * SUB, SUB)]
    for c in sent:
        c.wait_send()


def pair_sums(factor_a, factor_b, factor_c):
    dma = pltpu.SemaphoreType.DMA
    return pl.pallas_call(
        pair_kernel,
        out_shape=pltpu.VMEM((3, 32, 1024), jnp.float32),
        in_specs=[pl.BlockSpec(memory_space=pl.ANY)] * 3,
        out_specs=pl.BlockSpec(memory_space=pltpu.VMEM),
        scratch_shapes=[
            pltpu.VMEM((3, 1024, 1024), jnp.bfloat16),
            pltpu.VMEM((2, 3, 256, 1024), jnp.bfloat16),
            pltpu.VMEM((2, 3, 256, 1024), jnp.float32),
            pltpu.VMEM((2, 3, 256, 256), jnp.float32),
            pltpu.VMEM((3, 32, 1024), jnp.float32),
            pltpu.VMEM((2, 3, 3, 64, 1024), jnp.bfloat16),
            pltpu.VMEM((2, 3, 3, 64, 1024), jnp.bfloat16),
            pltpu.VMEM((2, 3, 3, 16, 1024), jnp.bfloat16),
            pltpu.VMEM((2, 3, 3, 16, 1024), jnp.bfloat16),
            dma((3,)), dma((2, 16, 3)), dma((2, 16, 3)), dma((2, 16)), dma((2, 16)),
            dma((2, 3)), dma((2, 3)), dma((2, 3, 4)), dma((2, 3, 4)),
            dma((2, 3, 3)), dma((2, 3, 3)), dma((2, 3, 3)), dma((2, 3, 3)),
        ],
        compiler_params=pltpu.CompilerParams(collective_id=0, has_side_effects=True, vmem_limit_bytes=56 * 1024 * 1024),
        cost_estimate=pl.CostEstimate(flops=6 * 2 * 512 * 1024 * 1024, bytes_accessed=1 << 20, transcendentals=0),
        name="pair_sums",
    )(factor_a, factor_b, factor_c)


def shards(factor_a, factor_b, factor_c):
    out = pair_sums(factor_a, factor_b, factor_c)
    return (NMAT * out[0], NMAT * out[1], NMAT * out[2])


def solution(mesh):
    specs = (P(("col", "row"), None),) * 3
    return jax.shard_map(shards, mesh=mesh, in_specs=specs, out_specs=specs, check_vma=False)
```

```python
import jax
import jax.numpy as jnp
from jax import lax
from jax.experimental import pallas as pl
from jax.experimental.pallas import tpu as pltpu
from jax.sharding import PartitionSpec as P

NMAT = 32
MESH = pl.DeviceIdType.MESH
SUB = 16
STEPS = 15


def gram(left, right):
    return lax.dot_general(left, right, (((1,), (1,)), ((), ())), preferred_element_type=jnp.float32)


def pair_kernel(
    a_hbm, b_hbm, c_hbm, *rest,
):
    outs = [rest[0].at[f] for f in range(3)]
    (jbuf, ibuf, acc, grams, trace, stage_b, recv_b, stage_a, recv_a,
    load_sem, z_send, z_recv, s_send, s_recv, ga_send, ga_recv, gb_send, gb_recv, rb_send, rb_recv, ra_send, ra_recv) = rest[1:]
    row, col = lax.axis_index("row"), lax.axis_index("col")
    z, core = row // 2, lax.rem(row, 2)
    x, y = col // 4, lax.rem(col, 4)
    sign = 1 - 2 * core
    z_next = (lax.rem(z + 1, 16) * 2 + core, col)
    z_prev = (lax.rem(z + 15, 16) * 2 + core, col)
    sibling = (z * 2 + 1 - core, col)
    x_fwd = (row, lax.rem(x + 4 + sign, 4) * 4 + y)
    x_back = (row, lax.rem(x + 4 - sign, 4) * 4 + y)
    y_fwd = (row, x * 4 + lax.rem(y + 4 + sign, 4))
    y_back = (row, x * 4 + lax.rem(y + 4 - sign, 4))
    x_far = (row, lax.rem(x + 2, 4) * 4 + y)
    y_far = (row, x * 4 + lax.rem(y + 2, 4))
    far = (x_far, y_far)
    first = ((x_fwd, x_back), (y_fwd, y_back))
    second = ((y_fwd, y_back), (x_fwd, x_back))

    factors = (a_hbm, b_hbm, c_hbm)
    barrier = pltpu.get_barrier_semaphore()
    partners = (z_next, z_prev, sibling, x_fwd, x_back, y_fwd, y_back, x_far, y_far)
    for p in partners:
        pl.semaphore_signal(barrier, inc=1, device_id=p, device_id_type=MESH)
    loads = [pltpu.make_async_copy(factors[f], jbuf.at[f, pl.ds(0, 2 * SUB)], load_sem.at[f]) for f in range(3)]
    for load in loads:
        load.start()
    pl.semaphore_wait(barrier, len(partners))

    sent = []

    def copy(src, dst, send, recv, device):
        return pltpu.make_async_remote_copy(src, dst, send, recv, device_id=device, device_id_type=MESH)

    def go(c):
        c.start()
        sent.append(c)

    def jrows(slot, n=SUB):
        return jbuf.at[:, pl.ds(slot * SUB, n)]

    def z_copy(k, f, d):
        if k <= 2:
            src = factors[f].at[pl.ds((k - 1 if d == 0 else 2 - k) * SUB, SUB)]
        else:
            src = jbuf.at[f, pl.ds((4 * (k - 2) + d) * SUB, SUB)]
        return copy(
            src, jbuf.at[f, pl.ds((4 * k + d) * SUB, SUB)],
            z_send.at[d, k, f], z_recv.at[d, k, f], (z_next, z_prev)[d],
        )

    def s_copy(k, d):
        return copy(jrows(4 * k + d), jrows(4 * k + 2 + d), s_send.at[d, k], s_recv.at[d, k], sibling)

    own_copy = copy(jrows(0, 2 * SUB), jrows(2, 2 * SUB), s_send.at[0, 0], s_recv.at[0, 0], sibling)

    def irows(t, slot):
        return ibuf.at[t, :, pl.ds(slot * SUB, SUB)]

    def ga_copy(t, kind):
        fwd, back = first[t]
        own = jrows(t)
        src, slot, device = ((own, 3, fwd), (own, 1, back), (irows(t, 3), 2, fwd))[kind]
        return copy(src, irows(t, slot), ga_send.at[t, kind], ga_recv.at[t, kind], device)

    def gb_copy(t, kind, a):
        fwd, back = second[t]
        own = jrows(t) if a == 0 else irows(t, a)
        src, b, device = ((own, 3, fwd), (own, 1, back), (irows(t, 12 + a), 2, fwd))[kind]
        return copy(src, irows(t, 4 * b + a), gb_send.at[t, kind, a], gb_recv.at[t, kind, a], device)

    def rb_copy(t, f, kind):
        fwd, back = second[t]
        return copy(stage_b.at[t, f, kind], recv_b.at[t, f, kind], rb_send.at[t, f, kind], rb_recv.at[t, f, kind], (fwd, back, fwd)[kind])

    def ra_copy(t, f, kind):
        fwd, back = first[t]
        device = (fwd, far[t], back)[kind]
        return copy(stage_a.at[t, f, kind], recv_a.at[t, f, kind], ra_send.at[t, f, kind], ra_recv.at[t, f, kind], device)

    def gram_item(t, group, f):
        def run():
            grams[t, f] = gram(ibuf[t, f], jbuf[f, pl.ds(group * 256, 256)])
        return run

    def apply_item(t, group, f):
        def run():
            hadam = (grams[t, (f + 1) % 3] * grams[t, (f + 2) % 3]).astype(jnp.bfloat16)
            term = jnp.dot(hadam, jbuf[f, pl.ds(group * 256, 256)], preferred_element_type=jnp.float32)
            if group > 0:
                term = acc[t, f] + term
            if group == 3:
                stage_b[t, f, 0] = term[128:192].astype(jnp.bfloat16)
                stage_b[t, f, 1] = term[192:256].astype(jnp.bfloat16)
                go(rb_copy(t, f, 0))
                acc[t, f, pl.ds(0, 128)] = term[0:128]
            else:
                acc[t, f] = term
        return run

    def wait_group(group):
        for k in range(4 * group, 4 * group + 4):
            if k == 0:
                own_copy.wait_recv()
            else:
                s_copy(k, 0).wait_recv()
                s_copy(k, 1).wait_recv()

    def unit_items(t, group):
        items = [gram_item(t, group, f) for f in range(3)] + [apply_item(t, group, f) for f in range(3)]
        return items

    for f in range(3):
        for d in range(2):
            go(z_copy(1, f, d))
    for load in loads:
        load.wait()
    for t in range(2):
        go(ga_copy(t, 0))
        go(ga_copy(t, 1))
    for f in range(3):
        for d in range(2):
            go(z_copy(2, f, d))
    for t in range(2):
        go(gb_copy(t, 0, 0))
        go(gb_copy(t, 1, 0))
    go(own_copy)
    for t in range(2):
        ibuf[t, :, pl.ds(0, SUB)] = jbuf[:, pl.ds(t * SUB, SUB)]

    def trace_terms():
        cubes = [jbuf[f, pl.ds(0, 32)].reshape(32, NMAT, NMAT) for f in range(3)]
        for f, spec in enumerate(("rjk,rki->rij", "rki,rij->rjk", "rij,rjk->rki")):
            data = jnp.einsum(spec, cubes[(f + 1) % 3], cubes[(f + 2) % 3] , preferred_element_type=jnp.float32)
            trace[f] = data.reshape(32, NMAT * NMAT)

    ready = {9: 0, 10: 1, 12: 2}
    queue = []

    def xy_events(k):
        if k == ga_at[0]:
            for t in range(2):
                ga_copy(t, 0).wait_recv()
                go(ga_copy(t, 2))
                go(gb_copy(t, 0, 3))
                go(gb_copy(t, 1, 3))
            for t in range(2):
                ga_copy(t, 1).wait_recv()
                go(gb_copy(t, 0, 1))
                go(gb_copy(t, 1, 1))
        if k == ga_at[1]:
            for t in range(2):
                ga_copy(t, 2).wait_recv()
                go(gb_copy(t, 0, 2))
                go(gb_copy(t, 1, 2))
        for a, when in gb_at:
            if k == when:
                for t in range(2):
                    gb_copy(t, 0, a).wait_recv()
                    go(gb_copy(t, 2, a))
        if k == i_at:
            for t in range(2):
                for a in range(4):
                    gb_copy(t, 1, a).wait_recv()
                    gb_copy(t, 2, a).wait_recv()

    ga_at, gb_at, i_at = (2, 4), ((0, 3), (3, 5), (1, 6), (2, 7)), 9
    for k in range(1, STEPS + 1):
        for f in range(3):
            for d in range(2):
                z_copy(k, f, d).wait_recv()
                if k + 2 <= STEPS:
                    go(z_copy(k + 2, f, d))
                if f == 2:
                    go(s_copy(k, d))
            if f == 0:
                xy_events(k)
                if k == 1:
                    trace_terms()
                if k in ready:
                    wait_group(ready[k])
                    queue.extend(unit_items(0, ready[k]) + unit_items(1, ready[k]))
            for _ in range(2):
                if queue:
                    queue.pop(0)()
    while queue:
        queue.pop(0)()
    wait_group(3)
    gathers = list(sent)
    del sent[:]
    for f in (1, 2):
        gram_item(0, 3, f)()
    apply_item(0, 3, 0)()
    for f in (1, 2):
        gram_item(1, 3, f)()
    apply_item(1, 3, 0)()
    for t in range(2):
        gram_item(t, 3, 0)()
        apply_item(t, 3, 1)()
    for t in range(2):
        apply_item(t, 3, 2)()

    def combine(t, f):
        rb_copy(t, f, 0).wait_recv()
        stage_b[t, f, 2] = (acc[t, f, pl.ds(64, 64)] + recv_b[t, f, 0].astype(jnp.float32)).astype(jnp.bfloat16)

    def second_step(t, f):
        rb_copy(t, f, 1).wait_recv()
        rb_copy(t, f, 2).wait_recv()
        total = acc[t, f, pl.ds(0, 64)] + recv_b[t, f, 1].astype(jnp.float32) + recv_b[t, f, 2].astype(jnp.float32)
        for kind, a in ((1, 2), (0, 1), (2, 3)):
            stage_a[t, f, kind] = total[SUB * a : SUB * a + SUB].astype(jnp.bfloat16)
            go(ra_copy(t, f, kind))
        acc[t, f, pl.ds(0, SUB)] = total[0:SUB]

    raws = list(sent)
    del sent[:]
    for f in range(2):
        for t in range(2):
            combine(t, f)
            rb_copy(t, f, 2).start()
            rb_copy(t, f, 1).start()
    for c in gathers:
        c.wait_send()
    for t in range(2):
        combine(t, 2)
        rb_copy(t, 0, 2).wait_send()
        rb_copy(t, 2, 2).start()
        rb_copy(t, 0, 1).wait_send()
        rb_copy(t, 2, 1).start()
    for f in range(3):
        for t in range(2):
            second_step(t, f)
    for f in (1, 2):
        for t in range(2):
            rb_copy(t, f, 2).wait_send()
            rb_copy(t, f, 1).wait_send()
    for c in raws:
        c.wait_send()
    for f, out_ref in enumerate(outs):
        for t in range(2):
            for kind in range(3):
                ra_copy(t, f, kind).wait_recv()
            received = [recv_a[t, f, kind].astype(jnp.float32) for kind in range(3)]
            summed = acc[t, f, pl.ds(0, SUB)] + received[0] + received[1] + received[2]
            out_ref[pl.ds(t * SUB, SUB)] = summed - trace[f, pl.ds(t * SUB, SUB)]
    for c in sent:
        c.wait_send()


def pair_sums(factor_a, factor_b, factor_c):
    dma = pltpu.SemaphoreType.DMA
    return pl.pallas_call(
        pair_kernel,
        out_shape=pltpu.VMEM((3, 32, 1024), jnp.float32),
        in_specs=[pl.BlockSpec(memory_space=pl.ANY)] * 3,
        out_specs=pl.BlockSpec(memory_space=pltpu.VMEM),
        scratch_shapes=[
            pltpu.VMEM((3, 1024, 1024), jnp.bfloat16),
            pltpu.VMEM((2, 3, 256, 1024), jnp.bfloat16),
            pltpu.VMEM((2, 3, 256, 1024), jnp.float32),
            pltpu.VMEM((2, 3, 256, 256), jnp.float32),
            pltpu.VMEM((3, 32, 1024), jnp.float32),
            pltpu.VMEM((2, 3, 3, 64, 1024), jnp.bfloat16),
            pltpu.VMEM((2, 3, 3, 64, 1024), jnp.bfloat16),
            pltpu.VMEM((2, 3, 3, 16, 1024), jnp.bfloat16),
            pltpu.VMEM((2, 3, 3, 16, 1024), jnp.bfloat16),
            dma((3,)), dma((2, 16, 3)), dma((2, 16, 3)), dma((2, 16)), dma((2, 16)),
            dma((2, 3)), dma((2, 3)), dma((2, 3, 4)), dma((2, 3, 4)),
            dma((2, 3, 3)), dma((2, 3, 3)), dma((2, 3, 3)), dma((2, 3, 3)),
        ],
        compiler_params=pltpu.CompilerParams(collective_id=0, has_side_effects=True, vmem_limit_bytes=56 * 1024 * 1024),
        cost_estimate=pl.CostEstimate(flops=6 * 2 * 512 * 1024 * 1024, bytes_accessed=1 << 20, transcendentals=0),
        name="pair_sums",
    )(factor_a, factor_b, factor_c)


def shards(factor_a, factor_b, factor_c):
    out = pair_sums(factor_a, factor_b, factor_c)
    return (NMAT * out[0], NMAT * out[1], NMAT * out[2])


def solution(mesh):
    specs = (P(("col", "row"), None),) * 3
    return jax.shard_map(shards, mesh=mesh, in_specs=specs, out_specs=specs, check_vma=False)
```

```python
import jax
import jax.numpy as jnp
from jax import lax
from jax.experimental import pallas as pl
from jax.experimental.pallas import tpu as pltpu
from jax.sharding import PartitionSpec as P

NMAT = 32
MESH = pl.DeviceIdType.MESH
SUB = 16
STEPS = 15


def gram(left, right):
    return lax.dot_general(left, right, (((1,), (1,)), ((), ())), preferred_element_type=jnp.float32)


def pair_kernel(
    a_hbm, b_hbm, c_hbm, *rest,
):
    outs = [rest[0].at[f] for f in range(3)]
    (jbuf, ibuf, acc, grams, trace, stage_b, recv_b, stage_a, recv_a,
    load_sem, z_send, z_recv, s_send, s_recv, ga_send, ga_recv, gb_send, gb_recv, rb_send, rb_recv, ra_send, ra_recv) = rest[1:]
    row, col = lax.axis_index("row"), lax.axis_index("col")
    z, core = row // 2, lax.rem(row, 2)
    x, y = col // 4, lax.rem(col, 4)
    sign = 1 - 2 * core
    z_next = (lax.rem(z + 1, 16) * 2 + core, col)
    z_prev = (lax.rem(z + 15, 16) * 2 + core, col)
    sibling = (z * 2 + 1 - core, col)
    x_fwd = (row, lax.rem(x + 4 + sign, 4) * 4 + y)
    x_back = (row, lax.rem(x + 4 - sign, 4) * 4 + y)
    y_fwd = (row, x * 4 + lax.rem(y + 4 + sign, 4))
    y_back = (row, x * 4 + lax.rem(y + 4 - sign, 4))
    x_far = (row, lax.rem(x + 2, 4) * 4 + y)
    y_far = (row, x * 4 + lax.rem(y + 2, 4))
    far = (x_far, y_far)
    first = ((x_fwd, x_back), (y_fwd, y_back))
    second = ((y_fwd, y_back), (x_fwd, x_back))

    factors = (a_hbm, b_hbm, c_hbm)
    barrier = pltpu.get_barrier_semaphore()
    partners = (z_next, z_prev, sibling, x_fwd, x_back, y_fwd, y_back, x_far, y_far)
    for p in partners:
        pl.semaphore_signal(barrier, inc=1, device_id=p, device_id_type=MESH)
    loads = [pltpu.make_async_copy(factors[f], jbuf.at[f, pl.ds(0, 2 * SUB)], load_sem.at[f]) for f in range(3)]
    for load in loads:
        load.start()
    pl.semaphore_wait(barrier, len(partners))

    sent = []

    def copy(src, dst, send, recv, device):
        return pltpu.make_async_remote_copy(src, dst, send, recv, device_id=device, device_id_type=MESH)

    def go(c):
        c.start()
        sent.append(c)

    def jrows(slot, n=SUB):
        return jbuf.at[:, pl.ds(slot * SUB, n)]

    def z_copy(k, f, d):
        if k <= 2:
            src = factors[f].at[pl.ds((k - 1 if d == 0 else 2 - k) * SUB, SUB)]
        else:
            src = jbuf.at[f, pl.ds((4 * (k - 2) + d) * SUB, SUB)]
        return copy(
            src, jbuf.at[f, pl.ds((4 * k + d) * SUB, SUB)],
            z_send.at[d, k, f], z_recv.at[d, k, f], (z_next, z_prev)[d],
        )

    def s_copy(k, d):
        return copy(jrows(4 * k + d), jrows(4 * k + 2 + d), s_send.at[d, k], s_recv.at[d, k], sibling)

    own_copy = copy(jrows(0, 2 * SUB), jrows(2, 2 * SUB), s_send.at[0, 0], s_recv.at[0, 0], sibling)

    def irows(t, slot):
        return ibuf.at[t, :, pl.ds(slot * SUB, SUB)]

    def ga_copy(t, kind):
        fwd, back = first[t]
        own = jrows(t)
        src, slot, device = ((own, 3, fwd), (own, 1, back), (irows(t, 3), 2, fwd))[kind]
        return copy(src, irows(t, slot), ga_send.at[t, kind], ga_recv.at[t, kind], device)

    def gb_copy(t, kind, a):
        fwd, back = second[t]
        own = jrows(t) if a == 0 else irows(t, a)
        src, b, device = ((own, 3, fwd), (own, 1, back), (irows(t, 12 + a), 2, fwd))[kind]
        return copy(src, irows(t, 4 * b + a), gb_send.at[t, kind, a], gb_recv.at[t, kind, a], device)

    def rb_copy(t, f, kind):
        fwd, back = second[t]
        return copy(stage_b.at[t, f, kind], recv_b.at[t, f, kind], rb_send.at[t, f, kind], rb_recv.at[t, f, kind], (fwd, back, fwd)[kind])

    def ra_copy(t, f, kind):
        fwd, back = first[t]
        device = (fwd, far[t], back)[kind]
        return copy(stage_a.at[t, f, kind], recv_a.at[t, f, kind], ra_send.at[t, f, kind], ra_recv.at[t, f, kind], device)

    def gram_item(t, group, f):
        def run():
            grams[t, f] = gram(ibuf[t, f], jbuf[f, pl.ds(group * 256, 256)])
        return run

    def apply_item(t, group, f):
        def run():
            hadam = (grams[t, (f + 1) % 3] * grams[t, (f + 2) % 3]).astype(jnp.bfloat16)
            term = jnp.dot(hadam, jbuf[f, pl.ds(group * 256, 256)], preferred_element_type=jnp.float32)
            if group > 0:
                term = acc[t, f] + term
            if group == 3:
                stage_b[t, f, 0] = term[128:192].astype(jnp.bfloat16)
                stage_b[t, f, 1] = term[192:256].astype(jnp.bfloat16)
                go(rb_copy(t, f, 0))
                acc[t, f, pl.ds(0, 128)] = term[0:128]
            else:
                acc[t, f] = term
        return run

    def wait_group(group):
        for k in range(4 * group, 4 * group + 4):
            if k == 0:
                own_copy.wait_recv()
            else:
                s_copy(k, 0).wait_recv()
                s_copy(k, 1).wait_recv()

    def unit_items(t, group):
        items = [gram_item(t, group, f) for f in range(3)] + [apply_item(t, group, f) for f in range(3)]
        return items

    for f in range(3):
        for d in range(2):
            go(z_copy(1, f, d))
    for load in loads:
        load.wait()
    for t in range(2):
        go(ga_copy(t, 0))
        go(ga_copy(t, 1))
    for f in range(3):
        for d in range(2):
            go(z_copy(2, f, d))
    for t in range(2):
        go(gb_copy(t, 0, 0))
        go(gb_copy(t, 1, 0))
    go(own_copy)
    for t in range(2):
        ibuf[t, :, pl.ds(0, SUB)] = jbuf[:, pl.ds(t * SUB, SUB)]

    def trace_terms():
        cubes = [jbuf[f, pl.ds(0, 32)].reshape(32, NMAT, NMAT) for f in range(3)]
        for f, spec in enumerate(("rjk,rki->rij", "rki,rij->rjk", "rij,rjk->rki")):
            data = jnp.einsum(spec, cubes[(f + 1) % 3], cubes[(f + 2) % 3] , preferred_element_type=jnp.float32)
            trace[f] = data.reshape(32, NMAT * NMAT)

    ready = {9: 0, 11: 1, 12: 2}
    queue = []

    def xy_events(k):
        if k == ga_at[0]:
            for t in range(2):
                ga_copy(t, 0).wait_recv()
                go(ga_copy(t, 2))
                go(gb_copy(t, 0, 3))
                go(gb_copy(t, 1, 3))
            for t in range(2):
                ga_copy(t, 1).wait_recv()
                go(gb_copy(t, 0, 1))
                go(gb_copy(t, 1, 1))
        if k == ga_at[1]:
            for t in range(2):
                ga_copy(t, 2).wait_recv()
                go(gb_copy(t, 0, 2))
                go(gb_copy(t, 1, 2))
        for a, when in gb_at:
            if k == when:
                for t in range(2):
                    gb_copy(t, 0, a).wait_recv()
                    go(gb_copy(t, 2, a))
        for t in range(2):
            if k == i_at + t:
                for a in range(4):
                    gb_copy(t, 1, a).wait_recv()
                    gb_copy(t, 2, a).wait_recv()

    ga_at, gb_at, i_at = (2, 4), ((0, 3), (3, 5), (1, 6), (2, 7)), 9
    for k in range(1, STEPS + 1):
        for f in range(3):
            for d in range(2):
                z_copy(k, f, d).wait_recv()
                if k + 2 <= STEPS:
                    go(z_copy(k + 2, f, d))
                if f == 2:
                    go(s_copy(k, d))
            if f == 0:
                xy_events(k)
                if k == 1:
                    trace_terms()
                if k in ready:
                    wait_group(ready[k])
                    queue.extend(unit_items(0, ready[k]) + unit_items(1, ready[k]))
            for _ in range(2):
                if queue:
                    queue.pop(0)()
    while queue:
        queue.pop(0)()
    wait_group(3)
    gathers = list(sent)
    del sent[:]
    for f in (1, 2):
        gram_item(0, 3, f)()
    apply_item(0, 3, 0)()
    for f in (1, 2):
        gram_item(1, 3, f)()
    apply_item(1, 3, 0)()
    for t in range(2):
        gram_item(t, 3, 0)()
        apply_item(t, 3, 1)()
    for t in range(2):
        apply_item(t, 3, 2)()

    def combine(t, f):
        rb_copy(t, f, 0).wait_recv()
        stage_b[t, f, 2] = (acc[t, f, pl.ds(64, 64)] + recv_b[t, f, 0].astype(jnp.float32)).astype(jnp.bfloat16)

    def second_step(t, f):
        rb_copy(t, f, 1).wait_recv()
        rb_copy(t, f, 2).wait_recv()
        total = acc[t, f, pl.ds(0, 64)] + recv_b[t, f, 1].astype(jnp.float32) + recv_b[t, f, 2].astype(jnp.float32)
        for kind, a in ((1, 2), (0, 1), (2, 3)):
            stage_a[t, f, kind] = total[SUB * a : SUB * a + SUB].astype(jnp.bfloat16)
            go(ra_copy(t, f, kind))
        acc[t, f, pl.ds(0, SUB)] = total[0:SUB]

    raws = list(sent)
    del sent[:]
    for f in range(2):
        for t in range(2):
            combine(t, f)
            rb_copy(t, f, 2).start()
            rb_copy(t, f, 1).start()
    for c in gathers:
        c.wait_send()
    for t in range(2):
        combine(t, 2)
        rb_copy(t, 0, 2).wait_send()
        rb_copy(t, 2, 2).start()
        rb_copy(t, 0, 1).wait_send()
        rb_copy(t, 2, 1).start()
    for f in range(3):
        for t in range(2):
            second_step(t, f)
    for f in (1, 2):
        for t in range(2):
            rb_copy(t, f, 2).wait_send()
            rb_copy(t, f, 1).wait_send()
    for c in raws:
        c.wait_send()
    for f, out_ref in enumerate(outs):
        for t in range(2):
            for kind in range(3):
                ra_copy(t, f, kind).wait_recv()
            received = [recv_a[t, f, kind].astype(jnp.float32) for kind in range(3)]
            summed = acc[t, f, pl.ds(0, SUB)] + received[0] + received[1] + received[2]
            out_ref[pl.ds(t * SUB, SUB)] = summed - trace[f, pl.ds(t * SUB, SUB)]
    for c in sent:
        c.wait_send()


def pair_sums(factor_a, factor_b, factor_c):
    dma = pltpu.SemaphoreType.DMA
    return pl.pallas_call(
        pair_kernel,
        out_shape=pltpu.VMEM((3, 32, 1024), jnp.float32),
        in_specs=[pl.BlockSpec(memory_space=pl.ANY)] * 3,
        out_specs=pl.BlockSpec(memory_space=pltpu.VMEM),
        scratch_shapes=[
            pltpu.VMEM((3, 1024, 1024), jnp.bfloat16),
            pltpu.VMEM((2, 3, 256, 1024), jnp.bfloat16),
            pltpu.VMEM((2, 3, 256, 1024), jnp.float32),
            pltpu.VMEM((2, 3, 256, 256), jnp.float32),
            pltpu.VMEM((3, 32, 1024), jnp.float32),
            pltpu.VMEM((2, 3, 3, 64, 1024), jnp.bfloat16),
            pltpu.VMEM((2, 3, 3, 64, 1024), jnp.bfloat16),
            pltpu.VMEM((2, 3, 3, 16, 1024), jnp.bfloat16),
            pltpu.VMEM((2, 3, 3, 16, 1024), jnp.bfloat16),
            dma((3,)), dma((2, 16, 3)), dma((2, 16, 3)), dma((2, 16)), dma((2, 16)),
            dma((2, 3)), dma((2, 3)), dma((2, 3, 4)), dma((2, 3, 4)),
            dma((2, 3, 3)), dma((2, 3, 3)), dma((2, 3, 3)), dma((2, 3, 3)),
        ],
        compiler_params=pltpu.CompilerParams(collective_id=0, has_side_effects=True, vmem_limit_bytes=56 * 1024 * 1024),
        cost_estimate=pl.CostEstimate(flops=6 * 2 * 512 * 1024 * 1024, bytes_accessed=1 << 20, transcendentals=0),
        name="pair_sums",
    )(factor_a, factor_b, factor_c)


def shards(factor_a, factor_b, factor_c):
    out = pair_sums(factor_a, factor_b, factor_c)
    return (NMAT * out[0], NMAT * out[1], NMAT * out[2])


def solution(mesh):
    specs = (P(("col", "row"), None),) * 3
    return jax.shard_map(shards, mesh=mesh, in_specs=specs, out_specs=specs, check_vma=False)
```
